32 devices in a mesh: groups: 2 (over y), ctx: 16 (over z, x, core).
Axes of the slice: x: 2, y: 2, z: 4, core: 2. Of those that a mesh axis runs over, the one named last changes fastest.
Arguments:
- queries: bfloat16 [16384, 2048], P(('groups', 'ctx')), parts along dimension 0, may hold values from -60 to 60
- keys: bfloat16 [16384, 512], P(('groups', 'ctx')), parts along dimension 0, may hold values from -30 to 30
- values: bfloat16 [16384, 512], P(('groups', 'ctx')), parts along dimension 0, may hold values from -24 to 24
- block_lengths: int32 [32], P(('groups', 'ctx')), parts along dimension 0, may hold values from 256 to 512, as said below
- out_weight: bfloat16 [2048, 4096], P(None, 'ctx'), may hold values from -0.125 to 0.125
Outputs:
- hidden_states: bfloat16 [16384, 4096], P(('groups', 'ctx')), parts along dimension 0
The draws below stay inside these ranges and needn't reach their ends.
There are 2 independent parts, one for each index of `groups`. The reference program is written for one: setup_inputs(seed, part) draws one part's arguments, and reference() takes and returns one part's arrays. A program takes and returns all parts, laid end to end along the dimension named above; an argument that names none is the same for every part. Nothing has to cross between parts.
Inputs may be any that keep to these rules, and one draw needn't show every extreme that they name: `block_lengths`: block 0 always holds 512 valid tokens.
All inputs are finite; a program needn't handle non-finite values.
Results may differ from the reference program's by a relative error of at most 0.0057.
Values may be sent and summed in bfloat16 or wider, within the bound.
A program may use at most 128 MiB of HBM per device.

```python
import math
import jax
import jax.numpy as jnp
from jax import lax

D = 4096
HQ = 16
HK = 4
HD = 128
BLK = 512
NBLK = 16
TOKENS = 8192


def key_field(key):
    entries = jnp.clip(jax.random.normal(jax.random.fold_in(key, 101), (TOKENS, HK * HD), jnp.float32), -6.0, 6.0)
    return entries


def draw_keys(key, part):
    return key_field(key).astype(jnp.bfloat16)


def draw_queries(key, part):
    entries = 1.5 * jnp.clip(jax.random.normal(jax.random.fold_in(key, 103), (TOKENS, HQ * HD), jnp.float32), -6.0, 6.0)
    return entries.astype(jnp.bfloat16)


def draw_block_lengths(key, part):
    drawn = jax.random.randint(jax.random.fold_in(key, 105), (NBLK,), BLK // 2, BLK + 1, dtype=jnp.int32)
    return jnp.where(jnp.arange(NBLK) == 0, BLK, drawn).astype(jnp.int32)


def level_of(own_key, dims, cuts, least, high):
    gain = 1.0
    for position, parts in cuts:
        draws = jax.random.uniform(jax.random.fold_in(jax.random.fold_in(own_key, 6), position), (parts,), jnp.float32, least / len(cuts), high / len(cuts))
        gain = gain * jnp.repeat(jnp.exp(draws), dims[position] // parts).reshape((-1,) + (1,) * (len(dims) - 1 - position))
    return gain


def noise(key, dims, deviation, most, split=(), kind=jnp.bfloat16):
    values = deviation * jax.random.normal(key, dims, jnp.float32)
    if split:
        values = values * level_of(key, dims, split, -0.22, 0.18)
    return jnp.clip(values, -most, most).astype(kind)


def setup_inputs(seed: int = 0, part: int = 0) -> dict:
    streams_of = jax.random.split(jax.random.key(seed), 6)
    own_keys = jax.random.split(jax.random.fold_in(streams_of[5], part), 6)
    return {
        "queries": draw_queries(jax.random.fold_in(jax.random.fold_in(streams_of[5], part), 71), part),
        "keys": draw_keys(jax.random.fold_in(jax.random.fold_in(streams_of[5], part), 71), part),
        "values": noise(own_keys[2], (TOKENS, HK * HD), 4.0, 24.0, ((0, 16),)),
        "block_lengths": draw_block_lengths(jax.random.fold_in(jax.random.fold_in(streams_of[5], part), 71), part),
        "out_weight": noise(streams_of[4], (HQ * HD, D), (HQ * HD) ** -0.5, 0.125, ((1, 16),)),
    }


def make_mask(row_count, valid_length, has_anchor):
    row_ids = jnp.arange(row_count)[:, None]
    col_ids = jnp.arange(row_count)[None, :]
    local_mask = (col_ids <= row_ids) & (col_ids < valid_length)
    anchor_mask = jnp.broadcast_to(has_anchor, (row_count, row_count))
    return jnp.concatenate([anchor_mask, local_mask], axis=1)

def attend_block(query_rows, key_rows, value_rows, anchor_keys, anchor_values, valid_length, has_anchor):
    row_count = query_rows.shape[0]
    key_heads = key_rows.shape[1] // HD
    group_size = query_rows.shape[1] // key_rows.shape[1]
    query_four = query_rows.astype(jnp.float32).reshape(row_count, key_heads, group_size, HD)
    key_three = jnp.concatenate([anchor_keys, key_rows], axis=0).astype(jnp.float32).reshape(2 * row_count, key_heads, HD)
    value_three = jnp.concatenate([anchor_values, value_rows], axis=0).astype(jnp.float32).reshape(2 * row_count, key_heads, HD)
    visible = make_mask(row_count, valid_length, has_anchor)
    scores = jnp.einsum('qhgd,khd->hgqk', query_four, key_three) / math.sqrt(HD)
    scores = jnp.where(visible, scores, -jnp.inf)
    row_top = lax.optimization_barrier(jnp.max(scores, axis=-1, keepdims=True))
    exponent = jnp.exp(scores - row_top)
    soft_weights = (exponent / lax.optimization_barrier(jnp.sum(exponent, axis=-1, keepdims=True))).astype(jnp.bfloat16)
    mixture = jnp.einsum('hgqk,khd->qhgd', soft_weights.astype(jnp.float32), value_three)
    return mixture.reshape(row_count, key_heads * group_size * HD).astype(jnp.bfloat16)

def reference(queries, keys, values, block_lengths, out_weight):
    anchor_keys = keys[:BLK]
    anchor_values = values[:BLK]

    def one_block(block_index):
        first_row = (block_index * BLK).astype(jnp.int32)
        query_rows = lax.dynamic_slice_in_dim(queries, first_row, BLK, 0)
        key_rows = lax.dynamic_slice_in_dim(keys, first_row, BLK, 0)
        value_rows = lax.dynamic_slice_in_dim(values, first_row, BLK, 0)
        mixture = attend_block(query_rows, key_rows, value_rows, anchor_keys, anchor_values, block_lengths[block_index], block_index > 0)
        return jnp.dot(mixture, out_weight, preferred_element_type=jnp.float32).astype(jnp.bfloat16)
    blocks = lax.map(one_block, jnp.arange(NBLK, dtype=jnp.int32))
    return blocks.reshape(TOKENS, D)
```

```python
import functools
import math

import jax
import jax.numpy as jnp
from jax import lax
from jax.experimental import pallas as pl
from jax.experimental.pallas import tpu as pltpu
from jax.sharding import PartitionSpec as P

HD = 128
MESH = pl.DeviceIdType.MESH
LOW = -1e30


def kernel(n, ctx_axis, length_ref, q_hbm, k_hbm, v_hbm, w_hbm, out_ref, q_ref, k_ref, v_ref, ak_ref, av_ref, wbuf,
           acc_ref, top_ref, sum_ref, mix_ref, ring_send, ring_recv, y_send, y_recv, sib_send, sib_recv,
           anchor_send, anchor_recv, local_sem):
    group = lax.axis_index("groups")
    me = lax.axis_index("ctx")
    chips = n // 2
    half = chips // 2
    core = me % 2
    chip = me // 2
    x = chip % 2
    z = chip // 2
    pos = (1 - x) * z + x * (chips - 1 - z)
    rows, width = w_hbm.shape
    tokens = q_ref.shape[0]
    kv_heads = k_ref.shape[1] // HD
    per_kv = q_ref.shape[1] // k_ref.shape[1]
    scale = math.log2(math.e) / math.sqrt(HD)

    def chip_at(p):
        p = (p + chips) % chips
        h = p // half
        return (1 - h) * 2 * p + h * (2 * (chips - 1 - p) + 1)

    right = (group, chip_at(pos + 1) * 2 + core)
    left = (group, chip_at(pos - 1) * 2 + core)
    other = (1 - group, me)
    sibling = (group, me + 1 - 2 * core)
    cross = (group, me + 2 - 4 * x)
    above = (group, (me + 4) % n)

    share = rows * 11 // 32 // 16 * 16
    mine = pl.ds(pl.multiple_of(group * share, 16), share)
    theirs = pl.ds(pl.multiple_of((1 - group) * share, 16), share)
    common = pl.ds(2 * share, rows - 2 * share)
    RIGHT, LEFT = 0, 1

    def origin(d, s, c):
        return chip_at(pos - s if d == RIGHT else pos + s) * 2 + c

    def remote(src, dst, send, recv, device):
        return pltpu.make_async_remote_copy(src_ref=src, dst_ref=dst, send_sem=send, recv_sem=recv,
                                            device_id=device, device_id_type=MESH)

    sent = []

    def ring_copy(d, s, piece):
        which = mine if piece == 0 else common
        o = origin(d, s - 1, core)
        src = (w_hbm if s == 1 else wbuf.at[o]).at[which]
        return remote(src, wbuf.at[o].at[which], ring_send.at[d, s - 1, piece], ring_recv.at[d, s - 1, piece],
                      right if d == RIGHT else left)

    def has(d, s, piece):
        if s < half:
            return True
        return s == half and piece == d

    def start(copy):
        copy.start()
        sent.append(copy)

    def sib_copy(d, s, part):
        which = (mine, common, theirs)[part]
        o = origin(d, s, core)
        return remote(wbuf.at[o].at[which], wbuf.at[o].at[which], sib_send.at[d, s, part], sib_recv.at[d, s, part], sibling)

    def y_copy(d, s):
        o = origin(d, s, core)
        return remote(wbuf.at[o].at[mine], wbuf.at[o].at[mine], y_send.at[d, s - 1], y_recv.at[d, s - 1], other)

    own_sib = remote(w_hbm, wbuf.at[me], sib_send.at[0, 0, 0], sib_recv.at[0, 0, 0], sibling)

    def serve_ring(s, piece):
        for d in (RIGHT, LEFT):
            if not has(d, s, piece):
                continue
            ring_copy(d, s, piece).wait_recv()
            if has(d, s + 1, piece):
                start(ring_copy(d, s + 1, piece))
            if piece == 0:
                start(y_copy(d, s))
            start(sib_copy(d, s, piece))

    def serve_y(s):
        for d in (RIGHT, LEFT):
            if has(d, s, 0):
                y_copy(d, s).wait_recv()
                start(sib_copy(d, s, 2))

    root = me == 0

    def anchor_copies(h):
        k = h * 2 // kv_heads
        cols = pl.ds(h * HD, HD)
        lead = (core == 0) & (x == k)
        z_cond = lead & (z < half - 1)
        x_cond = lead if k == 0 else (lead & (z > 0)) | root
        found = []
        for kind, (cond, device) in enumerate(((z_cond, above), (x_cond, cross), (core == 0, sibling))):
            for t, ref in enumerate((ak_ref, av_ref)):
                view = ref.at[:, cols]
                found.append((cond, remote(view, view, anchor_send.at[h, kind, t], anchor_recv.at[h, t], device)))
        return found

    def serve_anchor(h):
        @pl.when(me > 0)
        def _():
            for t, ref in enumerate((ak_ref, av_ref)):
                view = ref.at[:, pl.ds(h * HD, HD)]
                remote(view, view, anchor_send.at[h, 0, t], anchor_recv.at[h, t], sibling).wait_recv()
        send_anchor(h)

    def send_anchor(h):
        for cond, copy in anchor_copies(h):
            @pl.when(cond)
            def _():
                copy.start()

    loads = [
        pltpu.make_async_copy(k_hbm, k_ref, local_sem.at[0]),
        pltpu.make_async_copy(v_hbm, v_ref, local_sem.at[1]),
        pltpu.make_async_copy(q_hbm, q_ref, local_sem.at[2]),
        pltpu.make_async_copy(w_hbm, wbuf.at[me], local_sem.at[3]),
    ]
    for load in loads:
        load.start()
    root_loads = [
        pltpu.make_async_copy(k_hbm, ak_ref, local_sem.at[4]),
        pltpu.make_async_copy(v_hbm, av_ref, local_sem.at[5]),
    ]

    @pl.when(root)
    def _():
        for load in root_loads:
            load.start()

    barrier = pltpu.get_barrier_semaphore()
    for device in (right, left, other, sibling, cross):
        pl.semaphore_signal(barrier, inc=1, device_id=device, device_id_type=MESH)
    pl.semaphore_wait(barrier, 5)

    @pl.when(root)
    def _():
        for load in root_loads:
            load.wait()
        for h in range(kv_heads):
            send_anchor(h)

    for piece in (0, 1):
        for d in (RIGHT, LEFT):
            if has(d, 1, piece):
                start(ring_copy(d, 1, piece))
    start(own_sib)
    for load in loads:
        load.wait()

    def serve_anchor_beyond_root(h):
        @pl.when(me > 0)
        def _():
            for t, ref in enumerate((ak_ref, av_ref)):
                view = ref.at[:, pl.ds(h * HD, HD)]
                remote(view, view, anchor_send.at[h, 0, t], anchor_recv.at[h, t], sibling).wait_recv()
            send_anchor(h)

    last = length_ref[0] - 1
    block = tokens // 2

    def own_heads(j):
        cols = pl.ds(j * HD, HD)

        @pl.loop(0, per_kv)
        def _(i):
            h = j * per_kv + i
            head = pl.ds(pl.multiple_of(h * HD, HD), HD)
            for b in range(2):
                seen = block * (b + 1)
                rows_b = pl.ds(b * block, block)
                s = lax.dot_general(q_ref[rows_b, head], k_ref[pl.ds(0, seen), cols], (((1,), (1,)), ((), ())),
                                    preferred_element_type=jnp.float32)
                row = lax.broadcasted_iota(jnp.int32, (block, 1), 0) + b * block
                col = lax.broadcasted_iota(jnp.int32, (block, seen), 1)
                s = jnp.where(col <= jnp.minimum(row, last), s, LOW)
                top = jnp.max(s, axis=1, keepdims=True)
                e = jnp.exp2((s - top) * scale)
                top_ref[h, rows_b, :] = top
                sum_ref[h, rows_b, :] = jnp.sum(e, axis=1, keepdims=True)
                acc_ref[rows_b, head] = jnp.dot(e.astype(jnp.bfloat16), v_ref[pl.ds(0, seen), cols],
                                                preferred_element_type=jnp.float32)

    def anchor_heads(j):
        cols = pl.ds(j * HD, HD)

        @pl.when(me > 0)
        def _():
            @pl.loop(0, per_kv)
            def _(i):
                h = j * per_kv + i
                head = pl.ds(pl.multiple_of(h * HD, HD), HD)
                for b in range(2):
                    rows_b = pl.ds(b * block, block)
                    s = lax.dot_general(q_ref[rows_b, head], ak_ref[:, cols], (((1,), (1,)), ((), ())),
                                        preferred_element_type=jnp.float32)
                    old = top_ref[h, rows_b, :]
                    top = jnp.maximum(old, jnp.max(s, axis=1, keepdims=True))
                    e = jnp.exp2((s - top) * scale)
                    keep = jnp.exp2((old - top) * scale)
                    total = sum_ref[h, rows_b, :] * keep + jnp.sum(e, axis=1, keepdims=True)
                    mixed = acc_ref[rows_b, head] * keep + jnp.dot(e.astype(jnp.bfloat16), av_ref[:, cols],
                                                                   preferred_element_type=jnp.float32)
                    mix_ref[rows_b, head] = (mixed * (1.0 / total)).astype(jnp.bfloat16)

        @pl.when(me == 0)
        def _():
            @pl.loop(0, per_kv)
            def _(i):
                h = j * per_kv + i
                head = pl.ds(pl.multiple_of(h * HD, HD), HD)
                mix_ref[:, head] = (acc_ref[:, head] * (1.0 / sum_ref[h])).astype(jnp.bfloat16)

    def project(o):
        out_ref[:, pl.ds(pl.multiple_of(o * width, width), width)] = jnp.dot(
            mix_ref[...], wbuf[o], preferred_element_type=jnp.float32).astype(out_ref.dtype)

    def project_step(s):
        count = 2 if s == half else 4
        for d in (RIGHT, LEFT):
            for piece in range(3):
                if has(d, s, 1 if piece == 1 else 0):
                    sib_copy(d, s, piece).wait_recv()

        @pl.loop(0, count)
        def _(i):
            turn = 1 - 2 * (i // 2)
            project(chip_at(pos - turn * s) * 2 + (i + core) % 2)

    own_heads(0)
    for h in range(kv_heads // 2):
        serve_anchor_beyond_root(h)
    own_heads(1)
    for h in range(kv_heads // 2, kv_heads):
        serve_anchor_beyond_root(h)
    serve_ring(1, 0)
    own_heads(2)
    serve_ring(1, 1)
    own_heads(3)
    anchor_heads(0)
    serve_ring(2, 0)
    serve_y(1)
    anchor_heads(1)
    serve_ring(2, 1)
    anchor_heads(2)
    anchor_heads(3)
    serve_ring(3, 0)
    serve_y(2)
    project(me)
    own_sib.wait_recv()
    project(me + 1 - 2 * core)
    serve_ring(3, 1)
    project_step(1)
    serve_ring(4, 0)
    serve_y(3)
    project_step(2)
    serve_ring(4, 1)
    project_step(3)
    serve_y(4)
    project_step(4)
    for copy in sent:
        copy.wait_send()
    for h in range(kv_heads):
        for cond, copy in anchor_copies(h):
            @pl.when(cond)
            def _():
                copy.wait_send()


def fused(n, queries, keys, values, block_lengths, out_weight):
    tokens, features = queries.shape
    kv = keys.shape[1]
    heads = features // HD
    rows, width = out_weight.shape
    half = n // 4
    dma = pltpu.SemaphoreType.DMA
    return pl.pallas_call(
        functools.partial(kernel, n, "ctx"),
        out_shape=jax.ShapeDtypeStruct((tokens, n * width), jnp.bfloat16),
        in_specs=[pl.BlockSpec(memory_space=pltpu.SMEM)] + [pl.BlockSpec(memory_space=pl.ANY)] * 4,
        out_specs=pl.BlockSpec(memory_space=pltpu.VMEM),
        scratch_shapes=[
            pltpu.VMEM((tokens, features), jnp.bfloat16),
            pltpu.VMEM((tokens, kv), jnp.bfloat16),
            pltpu.VMEM((tokens, kv), jnp.bfloat16),
            pltpu.VMEM((tokens, kv), jnp.bfloat16),
            pltpu.VMEM((tokens, kv), jnp.bfloat16),
            pltpu.VMEM((n, rows, width), jnp.bfloat16),
            pltpu.VMEM((tokens, features), jnp.float32),
            pltpu.VMEM((heads, tokens, 1), jnp.float32),
            pltpu.VMEM((heads, tokens, 1), jnp.float32),
            pltpu.VMEM((tokens, features), jnp.bfloat16),
            dma((2, half, 2)),
            dma((2, half, 2)),
            dma((2, half)),
            dma((2, half)),
            dma((2, half + 1, 3)),
            dma((2, half + 1, 3)),
            dma((kv // HD, 3, 2)),
            dma((kv // HD, 2)),
            dma((6,)),
        ],
        compiler_params=pltpu.CompilerParams(
            collective_id=0, has_side_effects=True, vmem_limit_bytes=56 * 1024 * 1024
        ),
        name="attend_project",
    )(block_lengths, queries, keys, values, out_weight)


def broadcast(block, axis, source):
    block = jnp.where(lax.axis_index(axis) == source, block, jnp.zeros_like(block))
    return lax.psum(block, axis)


def make_mask(row_count, valid_length, has_anchor):
    row_ids = jnp.arange(row_count)[:, None]
    col_ids = jnp.arange(row_count)[None, :]
    local_mask = (col_ids <= row_ids) & (col_ids < valid_length)
    anchor_mask = jnp.broadcast_to(has_anchor, (row_count, row_count))
    return jnp.concatenate([anchor_mask, local_mask], axis=1)


def attend(query_rows, key_rows, value_rows, anchor_keys, anchor_values, valid_length, has_anchor):
    row_count = query_rows.shape[0]
    key_heads = key_rows.shape[1] // HD
    group_size = query_rows.shape[1] // key_rows.shape[1]
    query_stack = query_rows.reshape(row_count, key_heads, group_size, HD).transpose(1, 0, 2, 3)
    key_stack = (
        jnp.concatenate([anchor_keys, key_rows], axis=0)
        .reshape(2 * row_count, key_heads, HD)
        .transpose(1, 0, 2)
    )
    value_stack = (
        jnp.concatenate([anchor_values, value_rows], axis=0)
        .reshape(2 * row_count, key_heads, HD)
        .transpose(1, 0, 2)
    )
    visible = make_mask(row_count, valid_length, has_anchor)

    def one_head(operands):
        head_queries, head_keys, head_values = operands
        scores = jnp.einsum(
            "qgd,kd->gqk", head_queries, head_keys, preferred_element_type=jnp.float32
        ) / math.sqrt(HD)
        scores = jnp.where(visible[None], scores, -jnp.inf)
        row_top = jnp.max(scores, axis=-1, keepdims=True)
        exponent = jnp.exp(scores - row_top)
        soft_weights = (exponent / jnp.sum(exponent, axis=-1, keepdims=True)).astype(jnp.bfloat16)
        mixture = jnp.einsum(
            "gqk,kd->qgd", soft_weights, head_values, preferred_element_type=jnp.float32
        )
        return mixture.astype(jnp.bfloat16)

    stacked = lax.map(one_head, (query_stack, key_stack, value_stack))
    return stacked.transpose(1, 0, 2, 3).reshape(row_count, key_heads * group_size * HD)


def plain(queries, keys, values, block_lengths, out_weight):
    has_anchor = lax.axis_index("ctx") > 0
    anchor_keys, anchor_values = (broadcast(keys, "ctx", 0), broadcast(values, "ctx", 0))
    mixture = attend(
        queries, keys, values, anchor_keys, anchor_values, block_lengths[0], has_anchor
    )
    output = jnp.dot(
        mixture,
        lax.all_gather(out_weight, "ctx", axis=1, tiled=True),
        preferred_element_type=jnp.float32,
    )
    return output.astype(jnp.bfloat16)


def solution(mesh):
    n = mesh.shape["ctx"]

    def per_device(queries, keys, values, block_lengths, out_weight):
        if n == 16 and mesh.shape["groups"] == 2 and out_weight.shape[1] % 128 == 0:
            return fused(n, queries, keys, values, block_lengths, out_weight)
        return plain(queries, keys, values, block_lengths, out_weight)

    return jax.shard_map(
        per_device,
        mesh=mesh,
        in_specs=(
            P(("groups", "ctx"), None),
            P(("groups", "ctx"), None),
            P(("groups", "ctx"), None),
            P(("groups", "ctx")),
            P(None, "ctx"),
        ),
        out_specs=P(("groups", "ctx"), None),
        check_vma=False,
    )
```

```python
import functools
import math

import jax
import jax.numpy as jnp
from jax import lax
from jax.experimental import pallas as pl
from jax.experimental.pallas import tpu as pltpu
from jax.sharding import PartitionSpec as P

HD = 128
MESH = pl.DeviceIdType.MESH
LOW = -1e30


def kernel(n, ctx_axis, length_ref, q_hbm, k_hbm, v_hbm, w_hbm, out_ref, q_ref, k_ref, v_ref, ak_ref, av_ref, wbuf,
           acc_ref, top_ref, sum_ref, mix_ref, ring_send, ring_recv, y_send, y_recv, sib_send, sib_recv,
           anchor_send, anchor_recv, local_sem):
    group = lax.axis_index("groups")
    me = lax.axis_index("ctx")
    chips = n // 2
    half = chips // 2
    core = me % 2
    chip = me // 2
    x = chip % 2
    z = chip // 2
    pos = (1 - x) * z + x * (chips - 1 - z)
    rows, width = w_hbm.shape
    tokens = q_ref.shape[0]
    kv_heads = k_ref.shape[1] // HD
    per_kv = q_ref.shape[1] // k_ref.shape[1]
    scale = math.log2(math.e) / math.sqrt(HD)

    def chip_at(p):
        p = (p + chips) % chips
        h = p // half
        return (1 - h) * 2 * p + h * (2 * (chips - 1 - p) + 1)

    right = (group, chip_at(pos + 1) * 2 + core)
    left = (group, chip_at(pos - 1) * 2 + core)
    other = (1 - group, me)
    sibling = (group, me + 1 - 2 * core)
    cross = (group, me + 2 - 4 * x)
    above = (group, (me + 4) % n)

    share = rows * 11 // 32 // 16 * 16
    mine = pl.ds(pl.multiple_of(group * share, 16), share)
    theirs = pl.ds(pl.multiple_of((1 - group) * share, 16), share)
    common = pl.ds(2 * share, rows - 2 * share)
    RIGHT, LEFT = 0, 1

    def origin(d, s, c):
        return chip_at(pos - s if d == RIGHT else pos + s) * 2 + c

    def remote(src, dst, send, recv, device):
        return pltpu.make_async_remote_copy(src_ref=src, dst_ref=dst, send_sem=send, recv_sem=recv,
                                            device_id=device, device_id_type=MESH)

    sent = []

    def ring_copy(d, s, piece):
        which = mine if piece == 0 else common
        o = origin(d, s - 1, core)
        src = (w_hbm if s == 1 else wbuf.at[o]).at[which]
        return remote(src, wbuf.at[o].at[which], ring_send.at[d, s - 1, piece], ring_recv.at[d, s - 1, piece],
                      right if d == RIGHT else left)

    def has(d, s, piece):
        if s < half:
            return True
        return s == half and piece == d

    def start(copy):
        copy.start()
        sent.append(copy)

    def sib_copy(d, s, part):
        which = (mine, common, theirs)[part]
        o = origin(d, s, core)
        return remote(wbuf.at[o].at[which], wbuf.at[o].at[which], sib_send.at[d, s, part], sib_recv.at[d, s, part], sibling)

    def y_copy(d, s):
        o = origin(d, s, core)
        return remote(wbuf.at[o].at[mine], wbuf.at[o].at[mine], y_send.at[d, s - 1], y_recv.at[d, s - 1], other)

    own_sib = remote(w_hbm, wbuf.at[me], sib_send.at[0, 0, 0], sib_recv.at[0, 0, 0], sibling)

    def serve_ring(s, piece):
        for d in (RIGHT, LEFT):
            if not has(d, s, piece):
                continue
            ring_copy(d, s, piece).wait_recv()
            if has(d, s + 1, piece):
                start(ring_copy(d, s + 1, piece))
            if piece == 0:
                start(y_copy(d, s))
            start(sib_copy(d, s, piece))

    def serve_y(s):
        for d in (RIGHT, LEFT):
            if has(d, s, 0):
                y_copy(d, s).wait_recv()
                start(sib_copy(d, s, 2))

    root = me == 0
    chunks = 4
    chunk = tokens // chunks

    def anchor_copies(h):
        k = h * 2 // chunks
        part = pl.ds(h * chunk, chunk)
        lead = (core == 0) & (x == k)
        z_cond = lead & (z < half - 1)
        x_cond = lead if k == 0 else (lead & (z > 0)) | root
        found = []
        for kind, (cond, device) in enumerate(((z_cond, above), (x_cond, cross), (core == 0, sibling))):
            for t, ref in enumerate((ak_ref, av_ref)):
                view = ref.at[part, :]
                found.append((cond, remote(view, view, anchor_send.at[h, kind, t], anchor_recv.at[h, t], device)))
        return found

    def send_anchor(h):
        for cond, copy in anchor_copies(h):
            @pl.when(cond)
            def _():
                copy.start()

    loads = [
        pltpu.make_async_copy(k_hbm, k_ref, local_sem.at[0]),
        pltpu.make_async_copy(v_hbm, v_ref, local_sem.at[1]),
        pltpu.make_async_copy(q_hbm, q_ref, local_sem.at[2]),
        pltpu.make_async_copy(w_hbm, wbuf.at[me], local_sem.at[3]),
    ]
    for load in loads:
        load.start()
    root_loads = [
        pltpu.make_async_copy(k_hbm, ak_ref, local_sem.at[4]),
        pltpu.make_async_copy(v_hbm, av_ref, local_sem.at[5]),
    ]

    @pl.when(root)
    def _():
        for load in root_loads:
            load.start()

    barrier = pltpu.get_barrier_semaphore()
    for device in (right, left, other, sibling, cross):
        pl.semaphore_signal(barrier, inc=1, device_id=device, device_id_type=MESH)
    pl.semaphore_wait(barrier, 5)

    @pl.when(root)
    def _():
        for load in root_loads:
            load.wait()
        for h in (0, 2, 1, 3):
            send_anchor(h)

    firsts = [ring_copy(d, 1, piece) for piece in (0, 1) for d in (RIGHT, LEFT)] + [own_sib]
    sent.extend(firsts)

    @pl.when(core == 1)
    def _():
        for copy in firsts:
            copy.start()

    for load in loads:
        load.wait()

    def serve_anchor(h):
        @pl.when(me > 0)
        def _():
            for t, ref in enumerate((ak_ref, av_ref)):
                view = ref.at[pl.ds(h * chunk, chunk), :]
                remote(view, view, anchor_send.at[h, 0, t], anchor_recv.at[h, t], sibling).wait_recv()
            send_anchor(h)

    last = length_ref[0] - 1
    block = tokens // 2

    def own_heads(j):
        cols = pl.ds(j * HD, HD)

        @pl.loop(0, per_kv)
        def _(i):
            h = j * per_kv + i
            head = pl.ds(pl.multiple_of(h * HD, HD), HD)
            for b in range(2):
                seen = block * (b + 1)
                rows_b = pl.ds(b * block, block)
                s = lax.dot_general(q_ref[rows_b, head], k_ref[pl.ds(0, seen), cols], (((1,), (1,)), ((), ())),
                                    preferred_element_type=jnp.float32)
                row = lax.broadcasted_iota(jnp.int32, (block, 1), 0) + b * block
                col = lax.broadcasted_iota(jnp.int32, (block, seen), 1)
                s = jnp.where(col <= jnp.minimum(row, last), s, LOW)
                top = jnp.max(s, axis=1, keepdims=True)
                e = jnp.exp2((s - top) * scale)
                top_ref[h, rows_b, :] = top
                sum_ref[h, rows_b, :] = jnp.sum(e, axis=1, keepdims=True)
                acc_ref[rows_b, head] = jnp.dot(e.astype(jnp.bfloat16), v_ref[pl.ds(0, seen), cols],
                                                preferred_element_type=jnp.float32)

    def anchor_heads(j):
        cols = pl.ds(j * HD, HD)

        @pl.when(me > 0)
        def _():
            @pl.loop(0, per_kv)
            def _(i):
                h = j * per_kv + i
                head = pl.ds(pl.multiple_of(h * HD, HD), HD)
                for b in range(2):
                    rows_b = pl.ds(b * block, block)
                    s = lax.dot_general(q_ref[rows_b, head], ak_ref[:, cols], (((1,), (1,)), ((), ())),
                                        preferred_element_type=jnp.float32)
                    old = top_ref[h, rows_b, :]
                    top = jnp.maximum(old, jnp.max(s, axis=1, keepdims=True))
                    e = jnp.exp2((s - top) * scale)
                    keep = jnp.exp2((old - top) * scale)
                    total = sum_ref[h, rows_b, :] * keep + jnp.sum(e, axis=1, keepdims=True)
                    mixed = acc_ref[rows_b, head] * keep + jnp.dot(e.astype(jnp.bfloat16), av_ref[:, cols],
                                                                   preferred_element_type=jnp.float32)
                    mix_ref[rows_b, head] = (mixed * (1.0 / total)).astype(jnp.bfloat16)

        @pl.when(me == 0)
        def _():
            @pl.loop(0, per_kv)
            def _(i):
                h = j * per_kv + i
                head = pl.ds(pl.multiple_of(h * HD, HD), HD)
                mix_ref[:, head] = (acc_ref[:, head] * (1.0 / sum_ref[h])).astype(jnp.bfloat16)

    def project(o):
        out_ref[:, pl.ds(pl.multiple_of(o * width, width), width)] = jnp.dot(
            mix_ref[...], wbuf[o], preferred_element_type=jnp.float32).astype(out_ref.dtype)

    def project_step(s):
        count = 2 if s == half else 4
        for d in (RIGHT, LEFT):
            for piece in range(3):
                if has(d, s, 1 if piece == 1 else 0):
                    sib_copy(d, s, piece).wait_recv()

        @pl.loop(0, count)
        def _(i):
            turn = 1 - 2 * (i // 2)
            project(chip_at(pos - turn * s) * 2 + (i + core) % 2)

    own_heads(0)

    @pl.when(core == 0)
    def _():
        for k in (0, 1):
            @pl.when(x == k)
            def _():
                serve_anchor(2 * k)
                serve_anchor(2 * k + 1)
        for copy in firsts:
            copy.start()
    own_heads(1)
    serve_ring(1,0)

    @pl.when(core == 0)
    def _():
        for k in (0, 1):
            @pl.when(x != k)
            def _():
                serve_anchor(2 * k)
                serve_anchor(2 * k + 1)
    own_heads(2)
    serve_ring(1,1)
    own_heads(3)
    serve_ring(2,0)
    serve_y(1)

    @pl.when(core == 1)
    def _():
        for h in range(chunks):
            serve_anchor(h)

    anchor_heads(0)
    anchor_heads(1)
    serve_ring(2,1)
    anchor_heads(2)
    serve_ring(3,0)
    serve_y(2)
    anchor_heads(3)
    serve_ring(3,1)
    project(me)
    own_sib.wait_recv()
    project(me + 1 - 2 * core)
    project_step(1)
    serve_ring(4,0)
    serve_y(3)
    project_step(2)
    serve_ring(4,1)
    project_step(3)
    serve_y(4)
    project_step(4)
    for copy in sent:
        copy.wait_send()
    for h in range(chunks):
        for cond, copy in anchor_copies(h):
            @pl.when(cond)
            def _():
                copy.wait_send()


def fused(n, queries, keys, values, block_lengths, out_weight):
    tokens, features = queries.shape
    kv = keys.shape[1]
    heads = features // HD
    rows, width = out_weight.shape
    half = n // 4
    dma = pltpu.SemaphoreType.DMA
    return pl.pallas_call(
        functools.partial(kernel, n, "ctx"),
        out_shape=jax.ShapeDtypeStruct((tokens, n * width), jnp.bfloat16),
        in_specs=[pl.BlockSpec(memory_space=pltpu.SMEM)] + [pl.BlockSpec(memory_space=pl.ANY)] * 4,
        out_specs=pl.BlockSpec(memory_space=pltpu.VMEM),
        scratch_shapes=[
            pltpu.VMEM((tokens, features), jnp.bfloat16),
            pltpu.VMEM((tokens, kv), jnp.bfloat16),
            pltpu.VMEM((tokens, kv), jnp.bfloat16),
            pltpu.VMEM((tokens, kv), jnp.bfloat16),
            pltpu.VMEM((tokens, kv), jnp.bfloat16),
            pltpu.VMEM((n, rows, width), jnp.bfloat16),
            pltpu.VMEM((tokens, features), jnp.float32),
            pltpu.VMEM((heads, tokens, 1), jnp.float32),
            pltpu.VMEM((heads, tokens, 1), jnp.float32),
            pltpu.VMEM((tokens, features), jnp.bfloat16),
            dma((2, half, 2)),
            dma((2, half, 2)),
            dma((2, half)),
            dma((2, half)),
            dma((2, half + 1, 3)),
            dma((2, half + 1, 3)),
            dma((4, 3, 2)),
            dma((4, 2)),
            dma((6,)),
        ],
        compiler_params=pltpu.CompilerParams(
            collective_id=0, has_side_effects=True, vmem_limit_bytes=56 * 1024 * 1024
        ),
        name="attend_project",
    )(block_lengths, queries, keys, values, out_weight)


def broadcast(block, axis, source):
    block = jnp.where(lax.axis_index(axis) == source, block, jnp.zeros_like(block))
    return lax.psum(block, axis)


def make_mask(row_count, valid_length, has_anchor):
    row_ids = jnp.arange(row_count)[:, None]
    col_ids = jnp.arange(row_count)[None, :]
    local_mask = (col_ids <= row_ids) & (col_ids < valid_length)
    anchor_mask = jnp.broadcast_to(has_anchor, (row_count, row_count))
    return jnp.concatenate([anchor_mask, local_mask], axis=1)


def attend(query_rows, key_rows, value_rows, anchor_keys, anchor_values, valid_length, has_anchor):
    row_count = query_rows.shape[0]
    key_heads = key_rows.shape[1] // HD
    group_size = query_rows.shape[1] // key_rows.shape[1]
    query_stack = query_rows.reshape(row_count, key_heads, group_size, HD).transpose(1, 0, 2, 3)
    key_stack = (
        jnp.concatenate([anchor_keys, key_rows], axis=0)
        .reshape(2 * row_count, key_heads, HD)
        .transpose(1, 0, 2)
    )
    value_stack = (
        jnp.concatenate([anchor_values, value_rows], axis=0)
        .reshape(2 * row_count, key_heads, HD)
        .transpose(1, 0, 2)
    )
    visible = make_mask(row_count, valid_length, has_anchor)

    def one_head(operands):
        head_queries, head_keys, head_values = operands
        scores = jnp.einsum(
            "qgd,kd->gqk", head_queries, head_keys, preferred_element_type=jnp.float32
        ) / math.sqrt(HD)
        scores = jnp.where(visible[None], scores, -jnp.inf)
        row_top = jnp.max(scores, axis=-1, keepdims=True)
        exponent = jnp.exp(scores - row_top)
        soft_weights = (exponent / jnp.sum(exponent, axis=-1, keepdims=True)).astype(jnp.bfloat16)
        mixture = jnp.einsum(
            "gqk,kd->qgd", soft_weights, head_values, preferred_element_type=jnp.float32
        )
        return mixture.astype(jnp.bfloat16)

    stacked = lax.map(one_head, (query_stack, key_stack, value_stack))
    return stacked.transpose(1, 0, 2, 3).reshape(row_count, key_heads * group_size * HD)


def plain(queries, keys, values, block_lengths, out_weight):
    has_anchor = lax.axis_index("ctx") > 0
    anchor_keys, anchor_values = (broadcast(keys, "ctx", 0), broadcast(values, "ctx", 0))
    mixture = attend(
        queries, keys, values, anchor_keys, anchor_values, block_lengths[0], has_anchor
    )
    output = jnp.dot(
        mixture,
        lax.all_gather(out_weight, "ctx", axis=1, tiled=True),
        preferred_element_type=jnp.float32,
    )
    return output.astype(jnp.bfloat16)


def solution(mesh):
    n = mesh.shape["ctx"]

    def per_device(queries, keys, values, block_lengths, out_weight):
        if n == 16 and mesh.shape["groups"] == 2 and out_weight.shape[1] % 128 == 0:
            return fused(n, queries, keys, values, block_lengths, out_weight)
        return plain(queries, keys, values, block_lengths, out_weight)

    return jax.shard_map(
        per_device,
        mesh=mesh,
        in_specs=(
            P(("groups", "ctx"), None),
            P(("groups", "ctx"), None),
            P(("groups", "ctx"), None),
            P(("groups", "ctx")),
            P(None, "ctx"),
        ),
        out_specs=P(("groups", "ctx"), None),
        check_vma=False,
    )
```
